32 devices in a mesh: section: 4 (over x, core), kv: 8 (over z, y).
Axes of the slice: x: 2, y: 2, z: 4, core: 2. Of those that a mesh axis runs over, the one named last changes fastest.
Arguments:
- queries: bfloat16 [256, 8192], P(('section', 'kv')), may hold values from -72 to 72
- new_keys: bfloat16 [256, 1024], P(('section', 'kv')), may hold values from -6 to 6
- new_values: bfloat16 [256, 1024], P(('section', 'kv')), may hold values from -6 to 6
- prefix_keys: bfloat16 [32768, 1024], P(('section', 'kv')), may hold values from -20 to 20
- prefix_values: bfloat16 [32768, 1024], P(('section', 'kv')), may hold values from -6 to 6
- lengths: int32 [4], replicated, may hold values from 512 to 8192, as said below
Outputs:
- attended: bfloat16 [256, 8192], P(('section', 'kv'))
The draws below stay inside these ranges and needn't reach their ends.
Inputs may be any that keep to these rules, and one draw needn't show every extreme that they name: `lengths`: some section has 8192 live rows and another 8192 // 16.
All inputs are finite; a program needn't handle non-finite values.
Results may differ from the reference program's by a relative error of at most 0.005.
Values may be sent and summed in bfloat16 or wider, within the bound.
A program may use at most 256 MiB of HBM per device.

```python
import jax
import jax.numpy as jnp
from jax import lax

H = 64
KVH = 8
DH = 128
SECTIONS = 4
QROWS = 64
PREFIX = 8192


def draw_queries(key, part):
    first = jax.random.fold_in(jax.random.fold_in(key, 17), 0)
    values = 2.5 * jnp.clip(jax.random.normal(first, (SECTIONS * QROWS, H * DH), jnp.float32), -6.0, 6.0)
    return values.astype(jnp.bfloat16)


def draw_prefix_keys(key, part):
    first = jax.random.fold_in(jax.random.fold_in(key, 23), 0)
    values = jnp.clip(jax.random.normal(first, (SECTIONS * PREFIX, KVH * DH), jnp.float32), -6.0, 6.0)
    return values.astype(jnp.bfloat16)


def draw_lengths(key, part):
    first, second = jax.random.split(jax.random.fold_in(key, 31))
    lowest = PREFIX // 16
    values = jax.random.randint(first, (SECTIONS,), lowest, PREFIX + 1, dtype=jnp.int32)
    order = jax.random.permutation(second, SECTIONS)
    values = values.at[order[0]].set(PREFIX).at[order[1]].set(lowest)
    return values


def levels(rng, extent, cuts, least, top_value):
    def one(axis_at, shards_of):
        draws = jax.random.uniform(jax.random.fold_in(jax.random.fold_in(rng, 6), axis_at), (shards_of,), jnp.float32, least / len(cuts), top_value / len(cuts))
        return jnp.repeat(jnp.exp(draws), extent[axis_at] // shards_of).reshape((-1,) + (1,) * (len(extent) - axis_at - 1))

    loudness = one(*cuts[0])
    for cut in cuts[1:]:
        loudness = loudness * one(*cut)
    return loudness


def gaussian(key, dims, width, bound, cuts=(), kind=jnp.bfloat16):
    values = width * jax.random.normal(key, dims, jnp.float32)
    if cuts:
        values = values * levels(key, dims, cuts, -0.22, 0.18)
    return jnp.clip(values, -bound, bound).astype(kind)


def setup_inputs(seed: int = 0) -> dict:
    splits = jax.random.split(jax.random.key(seed), 7)
    queries = draw_queries(jax.random.fold_in(splits[6], 71), 0)
    new_keys = gaussian(splits[1], (SECTIONS * QROWS, KVH * DH), 1.0, 6.0, ((0, 32),))
    new_values = gaussian(splits[2], (SECTIONS * QROWS, KVH * DH), 1.0, 6.0, ((0, 32),))
    prefix_keys = draw_prefix_keys(jax.random.fold_in(splits[6], 71), 0)
    prefix_values = gaussian(splits[4], (SECTIONS * PREFIX, KVH * DH), 1.0, 6.0, ((0, 32),))
    lengths = draw_lengths(jax.random.fold_in(splits[6], 71), 0)
    return dict(queries=queries, new_keys=new_keys, new_values=new_values, prefix_keys=prefix_keys, prefix_values=prefix_values, lengths=lengths)


NEG = -1.0e30


def reference(queries, new_keys, new_values, prefix_keys, prefix_values, lengths):
    group_size = H // KVH
    scale = DH ** -0.5
    pieces = []
    for section_id in range(SECTIONS):
        grouped_query_rows = queries[section_id * QROWS:(section_id + 1) * QROWS].astype(jnp.float32).reshape(QROWS, KVH, group_size, DH)
        key_rows = jnp.concatenate([prefix_keys[section_id * PREFIX:(section_id + 1) * PREFIX], new_keys[section_id * QROWS:(section_id + 1) * QROWS]], axis=0)
        value_rows = jnp.concatenate([prefix_values[section_id * PREFIX:(section_id + 1) * PREFIX], new_values[section_id * QROWS:(section_id + 1) * QROWS]], axis=0)
        key_rows = key_rows.astype(jnp.float32).reshape(PREFIX + QROWS, KVH, DH)
        value_rows = value_rows.astype(jnp.float32).reshape(PREFIX + QROWS, KVH, DH)
        places = jnp.arange(PREFIX + QROWS, dtype=jnp.int32)
        row_ids = jnp.arange(QROWS, dtype=jnp.int32)
        allowed = jnp.where(places[None, :] < PREFIX, (places < lengths[section_id])[None, :], (places[None, :] - PREFIX) <= row_ids[:, None])

        def one_head(operands):
            query_head, key_head, value_head = operands
            scores = jnp.einsum("rgd,nd->grn", query_head, key_head, precision=lax.Precision.HIGHEST) * scale
            scores = jnp.where(allowed[None], scores, NEG)
            peaks = jnp.max(scores, axis=-1, keepdims=True)
            weights = jnp.exp(scores - peaks)
            totals = jnp.sum(weights, axis=-1)
            rounded = lax.optimization_barrier(weights.astype(jnp.bfloat16)).astype(jnp.float32)
            summed = jnp.einsum("grn,nd->grd", rounded, value_head, precision=lax.Precision.HIGHEST)
            return summed / totals[..., None]

        result = lax.map(one_head, (jnp.moveaxis(grouped_query_rows, 1, 0), jnp.moveaxis(key_rows, 1, 0), jnp.moveaxis(value_rows, 1, 0)))
        pieces.append(jnp.transpose(result, (2, 0, 1, 3)).reshape(QROWS, H * DH).astype(jnp.bfloat16))
    attention = jnp.concatenate(pieces, axis=0)
    return jnp.roll(attention, QROWS, axis=0)
```

```python
import functools

import jax
import jax.numpy as jnp
from jax import lax
from jax.experimental import pallas as pl
from jax.experimental.pallas import tpu as pltpu
from jax.sharding import PartitionSpec as P

H = 64
KVH = 8
DH = 128
G = H // KVH
LANES = 128
NEG = -1e30
HALVES = 2
LAG = 1
LOG2E = 1.4426950408889634
MESH = pl.DeviceIdType.MESH
F32 = jnp.float32
BF16 = jnp.bfloat16


def lane_of(stats, h):
    return jnp.broadcast_to(stats[:, h : h + 1], stats.shape)


def kernel(
    sections, outer, inner,
    lengths_ref, q_hbm, nk_hbm, nv_hbm, k_hbm, v_hbm, out_ref,
    nkbuf, nvbuf, kbuf, vbuf, qbuf, obuf, ostat, ybuf, ystat, cbuf, cstat, zbuf, zstat,
    local_sem, qz_send, qy_send, qf_send, q_recv,
    yo_send, ys_send, yo_recv, ys_recv, xo_send, xs_send, zo_send, zs_send, zo_recv, zs_recv,
):
    sec = lax.axis_index("section")
    me = lax.axis_index("kv")
    a = me // inner
    b = me % inner
    following = (sec + 1) % sections
    previous = (sec + sections - 1) % sections
    rows = q_hbm.shape[0]
    depth = k_hbm.shape[0]
    span = q_hbm.shape[1] // HALVES
    heads = H // HALVES

    def cut(hf):
        return pl.ds(hf * span, span)

    def outer_at(d):
        if outer & (outer - 1):
            return (a + d) % outer
        at, bit = 0, 1
        while bit < outer:
            at = at + ((a // bit + d // bit) % 2) * bit
            bit *= 2
        return at

    def outer_back(d):
        if outer & (outer - 1):
            return (a + outer - d) % outer
        return outer_at(d)

    def inner_at(e):
        return (b + e) % inner

    loads = [
        pltpu.make_async_copy(k_hbm, kbuf.at[pl.ds(0, depth)], local_sem.at[0]),
        pltpu.make_async_copy(v_hbm, vbuf.at[pl.ds(0, depth)], local_sem.at[1]),
        pltpu.make_async_copy(q_hbm, qbuf.at[me], local_sem.at[2]),
        pltpu.make_async_copy(nk_hbm, nkbuf, local_sem.at[3]),
        pltpu.make_async_copy(nv_hbm, nvbuf, local_sem.at[4]),
    ]
    for load in loads:
        load.start()

    barrier = pltpu.get_barrier_semaphore()
    peers = [(sec, outer_at(d) * inner + b) for d in range(1, outer)]
    peers += [(sec, a * inner + inner_at(e)) for e in range(1, inner)]
    peers += [(following, me), (previous, me)]
    for s_at, k_at in peers:
        pl.semaphore_signal(
            barrier, inc=1, device_id={"section": s_at, "kv": k_at}, device_id_type=MESH
        )
    pl.semaphore_wait(barrier, len(peers))

    sends = []

    def push(src, dst, send_sem, recv_sem, s_at, k_at):
        copy = pltpu.make_async_remote_copy(
            src_ref=src, dst_ref=dst, send_sem=send_sem, recv_sem=recv_sem,
            device_id={"section": s_at, "kv": k_at}, device_id_type=MESH,
        )
        copy.start()
        sends.append(copy)

    def arrived(dst, recv_sem):
        pltpu.make_async_copy(dst, dst, recv_sem).wait()

    for hf in range(HALVES):
        for e in range(1, inner):
            push(
                q_hbm.at[:, cut(hf)], qbuf.at[me, :, cut(hf)], qy_send.at[e, hf], q_recv.at[me, hf],
                sec, a * inner + inner_at(e),
            )
    for d in range(1, outer):
        for hf in range(HALVES):
            push(
                q_hbm.at[:, cut(hf)], qbuf.at[me, :, cut(hf)], qz_send.at[d, hf], q_recv.at[me, hf],
                sec, outer_at(d) * inner + b,
            )

    def forward(d, hf):
        slot = outer_back(d) * inner + b
        piece = qbuf.at[slot, :, cut(hf)]
        arrived(piece, q_recv.at[slot, hf])
        for e in range(1, inner):
            push(
                piece, piece, qf_send.at[d, e, hf], q_recv.at[slot, hf], sec, a * inner + inner_at(e)
            )

    limit = lengths_ref[sec] - me * depth
    place = lax.broadcasted_iota(jnp.int32, (1, depth), 1)
    bias = jnp.where(place < limit, 0.0, NEG).astype(F32)
    scale = (DH ** -0.5) * LOG2E
    count = inner * G * rows
    lane = lax.broadcasted_iota(jnp.int32, (rows, LANES), 1)
    sub = lax.broadcasted_iota(jnp.int32, (rows, LANES), 0)
    ones = jnp.ones((depth + LANES, LANES), BF16)

    def compute(zc, hf):
        own_bias = jnp.concatenate(
            [
                jnp.where(
                    (lane < rows) & (me * rows + lane <= (zc * inner + y) * rows + sub), 0.0, NEG
                ).astype(F32)
                for y in range(inner)
                for _ in range(G)
            ],
            0,
        )

        def one_head(g, stats):
            at = pl.multiple_of(g * DH, DH)
            k = kbuf[:, pl.ds(at, DH)]
            v = vbuf[:, pl.ds(at, DH)]
            q = jnp.concatenate(
                [
                    qbuf[zc * inner + y, :, pl.ds(pl.multiple_of(g * G * DH + h * DH, DH), DH)].astype(F32)
                    for y in range(inner)
                    for h in range(G)
                ],
                0,
            ).astype(BF16)
            s = lax.dot_general(q, k, (((1,), (1,)), ((), ())), preferred_element_type=F32)
            s_old = s[:, :depth] + bias
            s_own = s[:, depth:] + own_bias
            peak = jnp.maximum(
                jnp.max(s_old, axis=-1, keepdims=True), jnp.max(s_own, axis=-1, keepdims=True)
            )
            p = jnp.concatenate(
                [jnp.exp2((s_old - peak) * scale), jnp.exp2((s_own - peak) * scale)], 1
            ).astype(BF16)
            acc = jnp.dot(p, jnp.concatenate([v, ones], 1), preferred_element_type=F32)
            total = acc[:, DH:]
            o = acc[:, :DH] / total
            level = peak * scale + jnp.log2(total)
            stats = list(stats)
            for y in range(inner):
                for h in range(G):
                    base = (y * G + h) * rows
                    obuf[zc * inner + y, :, pl.ds(pl.multiple_of(g * G * DH + h * DH, DH), DH)] = o[
                        base : base + rows
                    ].astype(BF16)
                    stats[y] = jnp.where(lane == g * G + h, level[base : base + rows], stats[y])
            return tuple(stats)

        stats = lax.fori_loop(
            hf * (KVH // HALVES), (hf + 1) * (KVH // HALVES), one_head,
            tuple(jnp.zeros((rows, LANES), F32) for _ in range(inner)), unroll=KVH // HALVES
        )
        for y in range(inner):
            ostat[zc * inner + y, hf] = stats[y]

    def spread(zc, hf):
        for e in range(1, inner):
            target = a * inner + inner_at(e)
            slot = zc * inner + inner_at(e)
            push(
                obuf.at[slot, :, cut(hf)], ybuf.at[zc, b, :, cut(hf)],
                yo_send.at[zc, inner_at(e), hf], yo_recv.at[zc, b, hf], sec, target,
            )
            push(
                ostat.at[slot, hf], ystat.at[zc, b, hf],
                ys_send.at[zc, inner_at(e), hf], ys_recv.at[zc, b, hf], sec, target,
            )

    def deliver(hf):
        for e in range(inner):
            target = a * inner + inner_at(e)
            push(
                obuf.at[target, :, cut(hf)], zbuf.at[outer + b, :, cut(hf)],
                xo_send.at[inner_at(e), hf], zo_recv.at[outer + b, hf], following, target,
            )
            push(
                ostat.at[target, hf], zstat.at[outer + b, hf],
                xs_send.at[inner_at(e), hf], zs_recv.at[outer + b, hf], following, target,
            )

    def mix(hf, parts, levels, store):
        peak = functools.reduce(jnp.maximum, levels)
        shares = [jnp.exp2(level - peak) for level in levels]
        total = functools.reduce(jnp.add, shares)
        shares = [share / total for share in shares]
        for h in range(hf * heads, (hf + 1) * heads):
            cols = pl.ds(h * DH, DH)
            value = functools.reduce(
                jnp.add,
                [part[:, cols].astype(F32) * lane_of(share, h) for part, share in zip(parts, shares)],
            )
            store(cols, value.astype(BF16))
        return peak + jnp.log2(total)

    def combine(zc, hf):
        parts, levels = [obuf.at[zc * inner + b]], [ostat[zc * inner + b, hf]]
        for e in range(1, inner):
            at = inner_at(e)
            arrived(ybuf.at[zc, at, :, cut(hf)], yo_recv.at[zc, at, hf])
            arrived(ystat.at[zc, at, hf], ys_recv.at[zc, at, hf])
            parts.append(ybuf.at[zc, at])
            levels.append(ystat[zc, at, hf])

        def store(cols, value):
            cbuf[zc, :, cols] = value

        cstat[zc, hf] = mix(hf, parts, levels, store)
        target = zc * inner + b
        push(
            cbuf.at[zc, :, cut(hf)], zbuf.at[a, :, cut(hf)], zo_send.at[zc, hf], zo_recv.at[a, hf],
            following, target,
        )
        push(
            cstat.at[zc, hf], zstat.at[a, hf], zs_send.at[zc, hf], zs_recv.at[a, hf],
            following, target,
        )

    for load in loads:
        load.wait()
    pad = jnp.zeros((LANES - rows, kbuf.shape[1]), F32)
    kbuf[pl.ds(depth, LANES), :] = jnp.concatenate([nkbuf[...].astype(F32), pad], 0).astype(BF16)
    vbuf[pl.ds(depth, LANES), :] = jnp.concatenate([nvbuf[...].astype(F32), pad], 0).astype(BF16)
    steps = [(d, hf) for d in range(outer) for hf in range(HALVES)]
    for t, (d, hf) in enumerate(steps):
        zc = outer_back(d)
        if t + 1 < len(steps) and steps[t + 1][0] > 0:
            forward(*steps[t + 1])
        for e in range(1, inner):
            slot = zc * inner + inner_at(e)
            arrived(qbuf.at[slot, :, cut(hf)], q_recv.at[slot, hf])
        compute(zc, hf)
        if d > 0:
            spread(zc, hf)
        if t >= LAG and steps[t - LAG][0] > 0:
            combine(outer_back(steps[t - LAG][0]), steps[t - LAG][1])
    for hf in range(HALVES):
        deliver(hf)
    for d, hf in steps[len(steps) - LAG :]:
        combine(outer_back(d), hf)

    def store_out(cols, value):
        out_ref[:, cols] = value

    origins = [outer_at(d) for d in range(1, outer)] + [outer + y for y in range(inner)]
    for hf in range(HALVES):
        for at in origins:
            arrived(zbuf.at[at, :, cut(hf)], zo_recv.at[at, hf])
            arrived(zstat.at[at, hf], zs_recv.at[at, hf])
        mix(
            hf, [zbuf.at[at] for at in origins], [zstat[at, hf] for at in origins], store_out
        )
    for copy in sends:
        copy.wait_send()


def split_of(count):
    return 1 << ((count.bit_length() - 1) // 2)


def on_device(sections, count, queries, new_keys, new_values, prefix_keys, prefix_values, lengths):
    inner = split_of(count)
    outer = count // inner
    rows, width = queries.shape
    depth, kv_width = prefix_keys.shape
    vmem = pl.BlockSpec(memory_space=pltpu.VMEM)
    anywhere = pl.BlockSpec(memory_space=pltpu.HBM)
    dma = pltpu.SemaphoreType.DMA
    return pl.pallas_call(
        functools.partial(kernel, sections, outer, inner),
        out_shape=jax.ShapeDtypeStruct((rows, width), BF16),
        in_specs=[pl.BlockSpec(memory_space=pltpu.SMEM), anywhere, anywhere, anywhere, anywhere, anywhere],
        out_specs=vmem,
        scratch_shapes=[
            pltpu.VMEM((rows, kv_width), BF16),
            pltpu.VMEM((rows, kv_width), BF16),
            pltpu.VMEM((depth + LANES, kv_width), BF16),
            pltpu.VMEM((depth + LANES, kv_width), BF16),
            pltpu.VMEM((count, rows, width), BF16),
            pltpu.VMEM((count, rows, width), BF16),
            pltpu.VMEM((count, HALVES, rows, LANES), F32),
            pltpu.VMEM((outer, inner, rows, width), BF16),
            pltpu.VMEM((outer, inner, HALVES, rows, LANES), F32),
            pltpu.VMEM((outer, rows, width), BF16),
            pltpu.VMEM((outer, HALVES, rows, LANES), F32),
            pltpu.VMEM((outer + inner, rows, width), BF16),
            pltpu.VMEM((outer + inner, HALVES, rows, LANES), F32),
            dma((5,)),
            dma((outer, HALVES)),
            dma((inner, HALVES)),
            dma((outer, inner, HALVES)),
            dma((count, HALVES)),
            dma((outer, inner, HALVES)),
            dma((outer, inner, HALVES)),
            dma((outer, inner, HALVES)),
            dma((outer, inner, HALVES)),
            dma((inner, HALVES)),
            dma((inner, HALVES)),
            dma((outer, HALVES)),
            dma((outer, HALVES)),
            dma((outer + inner, HALVES)),
            dma((outer + inner, HALVES)),
        ],
        compiler_params=pltpu.CompilerParams(
            collective_id=0, has_side_effects=True, vmem_limit_bytes=56 << 20
        ),
        name="section_attention",
    )(lengths, queries, new_keys, new_values, prefix_keys, prefix_values)


def solution(mesh):
    return jax.shard_map(
        functools.partial(on_device, mesh.shape["section"], mesh.shape["kv"]),
        mesh=mesh,
        in_specs=(
            P(("section", "kv"), None),
            P(("section", "kv"), None),
            P(("section", "kv"), None),
            P(("section", "kv"), None),
            P(("section", "kv"), None),
            P(),
        ),
        out_specs=P(("section", "kv"), None),
        check_vma=False,
    )
```

```python
import functools

import jax
import jax.numpy as jnp
from jax import lax
from jax.experimental import pallas as pl
from jax.experimental.pallas import tpu as pltpu
from jax.sharding import PartitionSpec as P

H = 64
KVH = 8
DH = 128
G = H // KVH
LANES = 128
NEG = -1e30
HALVES = 2
LAG = 2
LOG2E = 1.4426950408889634
MESH = pl.DeviceIdType.MESH
F32 = jnp.float32
BF16 = jnp.bfloat16


def line_order(at, outer):
    near = sorted(range(outer), key=lambda q: (abs(q - at), abs(2 * q + 1 - outer)))
    if len(near) > 2 and 2 * at + 1 != outer:
        near.sort(key=lambda q: 0 if q == at else 1 if q == at ^ 1 else 2 + abs(q - at))
    return near


def lane_of(stats, h):
    return jnp.broadcast_to(stats[:, h : h + 1], stats.shape)


def kernel(
    sections, outer, inner,
    lengths_ref, q_hbm, nk_hbm, nv_hbm, k_hbm, v_hbm, out_ref,
    nkbuf, nvbuf, kbuf, vbuf, qbuf, obuf, ostat, ybuf, ystat, cbuf, cstat, zbuf, zstat,
    local_sem, qz_send, qr_send, qy_send, qf_send, q_recv,
    yo_send, ys_send, yo_recv, ys_recv, xo_send, xs_send, zo_send, zs_send, zo_recv, zs_recv,
):
    sec = lax.axis_index("section")
    me = lax.axis_index("kv")
    a = me // inner
    b = me % inner
    following = (sec + 1) % sections
    previous = (sec + sections - 1) % sections
    rows = q_hbm.shape[0]
    depth = k_hbm.shape[0]
    span = q_hbm.shape[1] // HALVES
    heads = H // HALVES

    def cut(hf):
        return pl.ds(hf * span, span)

    table = [line_order(at, outer) for at in range(outer)]

    def outer_at(d):
        at = table[0][d]
        for k in range(1, outer):
            at = jnp.where(a == k, table[k][d], at)
        return at

    def side_of(step):
        return (a + step >= 0) & (a + step < outer)

    def inner_at(e):
        return (b + e) % inner

    loads = [
        pltpu.make_async_copy(k_hbm, kbuf.at[pl.ds(0, depth)], local_sem.at[0]),
        pltpu.make_async_copy(v_hbm, vbuf.at[pl.ds(0, depth)], local_sem.at[1]),
        pltpu.make_async_copy(q_hbm, qbuf.at[me], local_sem.at[2]),
        pltpu.make_async_copy(nk_hbm, nkbuf, local_sem.at[3]),
        pltpu.make_async_copy(nv_hbm, nvbuf, local_sem.at[4]),
    ]
    for load in loads:
        load.start()

    barrier = pltpu.get_barrier_semaphore()
    peers = [(sec, a * inner + inner_at(e)) for e in range(1, inner)]
    peers += [(following, me), (previous, me)]
    for s_at, k_at in peers:
        pl.semaphore_signal(
            barrier, inc=1, device_id={"section": s_at, "kv": k_at}, device_id_type=MESH
        )
    for step in (1, -1):

        @pl.when(side_of(step))
        def _(step=step):
            pl.semaphore_signal(
                barrier, inc=1, device_id={"section": sec, "kv": me + step * inner}, device_id_type=MESH
            )

    lines = side_of(1).astype(jnp.int32) + side_of(-1).astype(jnp.int32)
    pl.semaphore_wait(barrier, len(peers) + lines)

    sends = []

    def push(src, dst, send_sem, recv_sem, s_at, k_at, when=None):
        copy = pltpu.make_async_remote_copy(
            src_ref=src, dst_ref=dst, send_sem=send_sem, recv_sem=recv_sem,
            device_id={"section": s_at, "kv": k_at}, device_id_type=MESH,
        )
        if when is None:
            copy.start()
        else:
            pl.when(when)(copy.start)
        sends.append((copy, when))

    def arrived(dst, recv_sem):
        pltpu.make_async_copy(dst, dst, recv_sem).wait()

    for hf in range(HALVES):
        for e in range(1, inner):
            push(
                q_hbm.at[:, cut(hf)], qbuf.at[me, :, cut(hf)], qy_send.at[e, hf], q_recv.at[me, hf],
                sec, a * inner + inner_at(e),
            )
    for hf in range(HALVES):
        for i, step in enumerate((1, -1)):
            push(
                q_hbm.at[:, cut(hf)], qbuf.at[me, :, cut(hf)], qz_send.at[i, hf], q_recv.at[me, hf],
                sec, jnp.clip(a + step, 0, outer - 1) * inner + b, side_of(step),
            )

    def forward(d, hf):
        zs = outer_at(d)
        slot = zs * inner + b
        piece = qbuf.at[slot, :, cut(hf)]
        arrived(piece, q_recv.at[slot, hf])
        for i, step in enumerate((1, -1)):
            onward = side_of(step) & (zs < a if step > 0 else zs > a)
            push(
                piece, piece, qr_send.at[d, i, hf], q_recv.at[slot, hf],
                sec, jnp.clip(a + step, 0, outer - 1) * inner + b, onward,
            )
        for e in range(1, inner):
            push(
                piece, piece, qf_send.at[d, e, hf], q_recv.at[slot, hf], sec, a * inner + inner_at(e)
            )

    limit = lengths_ref[sec] - me * depth
    place = lax.broadcasted_iota(jnp.int32, (1, depth), 1)
    bias = jnp.where(place < limit, 0.0, NEG).astype(F32)
    scale = (DH ** -0.5) * LOG2E
    count = inner * G * rows
    lane = lax.broadcasted_iota(jnp.int32, (rows, LANES), 1)
    sub = lax.broadcasted_iota(jnp.int32, (rows, LANES), 0)
    ones = jnp.ones((depth + LANES, LANES), BF16)

    def compute(zc, hf):
        own_bias = jnp.concatenate(
            [
                jnp.where(
                    (lane < rows) & (me * rows + lane <= (zc * inner + y) * rows + sub), 0.0, NEG
                ).astype(F32)
                for y in range(inner)
                for _ in range(G)
            ],
            0,
        )

        def one_head(g, stats):
            at = pl.multiple_of(g * DH, DH)
            k = kbuf[:, pl.ds(at, DH)]
            v = vbuf[:, pl.ds(at, DH)]
            q = jnp.concatenate(
                [
                    qbuf[zc * inner + y, :, pl.ds(pl.multiple_of(g * G * DH + h * DH, DH), DH)].astype(F32)
                    for y in range(inner)
                    for h in range(G)
                ],
                0,
            ).astype(BF16)
            s = lax.dot_general(q, k, (((1,), (1,)), ((), ())), preferred_element_type=F32)
            s_old = s[:, :depth] + bias
            s_own = s[:, depth:] + own_bias
            peak = jnp.maximum(
                jnp.max(s_old, axis=-1, keepdims=True), jnp.max(s_own, axis=-1, keepdims=True)
            )
            p = jnp.concatenate(
                [jnp.exp2((s_old - peak) * scale), jnp.exp2((s_own - peak) * scale)], 1
            ).astype(BF16)
            acc = jnp.dot(p, jnp.concatenate([v, ones], 1), preferred_element_type=F32)
            total = acc[:, DH:]
            o = acc[:, :DH] / total
            level = peak * scale + jnp.log2(total)
            stats = list(stats)
            for y in range(inner):
                for h in range(G):
                    base = (y * G + h) * rows
                    obuf[zc * inner + y, :, pl.ds(pl.multiple_of(g * G * DH + h * DH, DH), DH)] = o[
                        base : base + rows
                    ].astype(BF16)
                    stats[y] = jnp.where(lane == g * G + h, level[base : base + rows], stats[y])
            return tuple(stats)

        stats = lax.fori_loop(
            hf * (KVH // HALVES), (hf + 1) * (KVH // HALVES), one_head,
            tuple(jnp.zeros((rows, LANES), F32) for _ in range(inner)), unroll=KVH // HALVES
        )
        for y in range(inner):
            ostat[zc * inner + y, hf] = stats[y]

    def spread(zc, hf):
        for e in range(1, inner):
            target = a * inner + inner_at(e)
            slot = zc * inner + inner_at(e)
            push(
                obuf.at[slot, :, cut(hf)], ybuf.at[zc, b, :, cut(hf)],
                yo_send.at[zc, inner_at(e), hf], yo_recv.at[zc, b, hf], sec, target,
            )
            push(
                ostat.at[slot, hf], ystat.at[zc, b, hf],
                ys_send.at[zc, inner_at(e), hf], ys_recv.at[zc, b, hf], sec, target,
            )

    def deliver(hf):
        for e in range(inner):
            target = a * inner + inner_at(e)
            push(
                obuf.at[target, :, cut(hf)], zbuf.at[outer + b, :, cut(hf)],
                xo_send.at[inner_at(e), hf], zo_recv.at[outer + b, hf], following, target,
            )
            push(
                ostat.at[target, hf], zstat.at[outer + b, hf],
                xs_send.at[inner_at(e), hf], zs_recv.at[outer + b, hf], following, target,
            )

    def mix(hf, parts, levels, store):
        peak = functools.reduce(jnp.maximum, levels)
        shares = [jnp.exp2(level - peak) for level in levels]
        total = functools.reduce(jnp.add, shares)
        shares = [share / total for share in shares]
        for h in range(hf * heads, (hf + 1) * heads):
            cols = pl.ds(h * DH, DH)
            value = functools.reduce(
                jnp.add,
                [part[:, cols].astype(F32) * lane_of(share, h) for part, share in zip(parts, shares)],
            )
            store(cols, value.astype(BF16))
        return peak + jnp.log2(total)

    def combine(zc, hf):
        parts, levels = [obuf.at[zc * inner + b]], [ostat[zc * inner + b, hf]]
        for e in range(1, inner):
            at = inner_at(e)
            arrived(ybuf.at[zc, at, :, cut(hf)], yo_recv.at[zc, at, hf])
            arrived(ystat.at[zc, at, hf], ys_recv.at[zc, at, hf])
            parts.append(ybuf.at[zc, at])
            levels.append(ystat[zc, at, hf])

        def store(cols, value):
            cbuf[zc, :, cols] = value

        cstat[zc, hf] = mix(hf, parts, levels, store)
        target = zc * inner + b
        push(
            cbuf.at[zc, :, cut(hf)], zbuf.at[a, :, cut(hf)], zo_send.at[zc, hf], zo_recv.at[a, hf],
            following, target,
        )
        push(
            cstat.at[zc, hf], zstat.at[a, hf], zs_send.at[zc, hf], zs_recv.at[a, hf],
            following, target,
        )

    for load in loads:
        load.wait()
    pad = jnp.zeros((LANES - rows, kbuf.shape[1]), F32)
    kbuf[pl.ds(depth, LANES), :] = jnp.concatenate([nkbuf[...].astype(F32), pad], 0).astype(BF16)
    vbuf[pl.ds(depth, LANES), :] = jnp.concatenate([nvbuf[...].astype(F32), pad], 0).astype(BF16)
    work = []
    for d in range(1, outer):
        work += [(forward, d, hf) for hf in range(HALVES)]
        if d <= HALVES:
            work.append((None, 0, d - 1))
    work += [(None, 0, hf) for hf in range(outer - 1, HALVES)]
    for d in [*range(2, outer), 1]:
        work += [(None, d, hf) for hf in range(HALVES)]
    done = []
    for act, d, hf in work:
        if act is not None:
            act(d, hf)
            continue
        zc = outer_at(d)
        for e in range(1, inner):
            slot = zc * inner + inner_at(e)
            arrived(qbuf.at[slot, :, cut(hf)], q_recv.at[slot, hf])
        compute(zc, hf)
        if d > 0:
            spread(zc, hf)
            done.append((zc, hf))
            if len(done) > LAG:
                combine(*done.pop(0))
    for hf in range(HALVES):
        deliver(hf)
    for zc, hf in done:
        combine(zc, hf)

    def store_out(cols, value):
        out_ref[:, cols] = value

    origins = [outer_at(d) for d in range(1, outer)] + [outer + y for y in range(inner)]
    for hf in range(HALVES):
        for at in origins:
            arrived(zbuf.at[at, :, cut(hf)], zo_recv.at[at, hf])
            arrived(zstat.at[at, hf], zs_recv.at[at, hf])
        mix(
            hf, [zbuf.at[at] for at in origins], [zstat[at, hf] for at in origins], store_out
        )
    for copy, when in sends:
        if when is None:
            copy.wait_send()
        else:
            pl.when(when)(copy.wait_send)


def split_of(count):
    return 1 << ((count.bit_length() - 1) // 2)


def on_device(sections, count, queries, new_keys, new_values, prefix_keys, prefix_values, lengths):
    inner = split_of(count)
    outer = count // inner
    rows, width = queries.shape
    depth, kv_width = prefix_keys.shape
    vmem = pl.BlockSpec(memory_space=pltpu.VMEM)
    anywhere = pl.BlockSpec(memory_space=pltpu.HBM)
    dma = pltpu.SemaphoreType.DMA
    return pl.pallas_call(
        functools.partial(kernel, sections, outer, inner),
        out_shape=jax.ShapeDtypeStruct((rows, width), BF16),
        in_specs=[pl.BlockSpec(memory_space=pltpu.SMEM), anywhere, anywhere, anywhere, anywhere, anywhere],
        out_specs=vmem,
        scratch_shapes=[
            pltpu.VMEM((rows, kv_width), BF16),
            pltpu.VMEM((rows, kv_width), BF16),
            pltpu.VMEM((depth + LANES, kv_width), BF16),
            pltpu.VMEM((depth + LANES, kv_width), BF16),
            pltpu.VMEM((count, rows, width), BF16),
            pltpu.VMEM((count, rows, width), BF16),
            pltpu.VMEM((count, HALVES, rows, LANES), F32),
            pltpu.VMEM((outer, inner, rows, width), BF16),
            pltpu.VMEM((outer, inner, HALVES, rows, LANES), F32),
            pltpu.VMEM((outer, rows, width), BF16),
            pltpu.VMEM((outer, HALVES, rows, LANES), F32),
            pltpu.VMEM((outer + inner, rows, width), BF16),
            pltpu.VMEM((outer + inner, HALVES, rows, LANES), F32),
            dma((5,)),
            dma((2, HALVES)),
            dma((outer, 2, HALVES)),
            dma((inner, HALVES)),
            dma((outer, inner, HALVES)),
            dma((count, HALVES)),
            dma((outer, inner, HALVES)),
            dma((outer, inner, HALVES)),
            dma((outer, inner, HALVES)),
            dma((outer, inner, HALVES)),
            dma((inner, HALVES)),
            dma((inner, HALVES)),
            dma((outer, HALVES)),
            dma((outer, HALVES)),
            dma((outer + inner, HALVES)),
            dma((outer + inner, HALVES)),
        ],
        compiler_params=pltpu.CompilerParams(
            collective_id=0, has_side_effects=True, vmem_limit_bytes=56 << 20
        ),
        name="section_attention",
    )(lengths, queries, new_keys, new_values, prefix_keys, prefix_values)


def solution(mesh):
    return jax.shard_map(
        functools.partial(on_device, mesh.shape["section"], mesh.shape["kv"]),
        mesh=mesh,
        in_specs=(
            P(("section", "kv"), None),
            P(("section", "kv"), None),
            P(("section", "kv"), None),
            P(("section", "kv"), None),
            P(("section", "kv"), None),
            P(),
        ),
        out_specs=P(("section", "kv"), None),
        check_vma=False,
    )
```

```python
import functools

import jax
import jax.numpy as jnp
from jax import lax
from jax.experimental import pallas as pl
from jax.experimental.pallas import tpu as pltpu
from jax.sharding import PartitionSpec as P

H = 64
KVH = 8
DH = 128
G = H // KVH
LANES = 128
NEG = -1e30
HALVES = 2
LAG = 2
LOG2E = 1.4426950408889634
MESH = pl.DeviceIdType.MESH
F32 = jnp.float32
BF16 = jnp.bfloat16


def line_order(at, outer):
    near = sorted(range(outer), key=lambda q: (abs(q - at), abs(2 * q + 1 - outer)))
    if len(near) > 2 and 2 * at + 1 != outer:
        near.sort(key=lambda q: 0 if q == at else 1 if q == at ^ 1 else 2 + abs(q - at))
    return near


def lane_of(stats, h):
    return jnp.broadcast_to(stats[:, h : h + 1], stats.shape)


def kernel(
    sections, outer, inner,
    lengths_ref, q_hbm, nk_hbm, nv_hbm, k_hbm, v_hbm, out_ref,
    nkbuf, nvbuf, kbuf, vbuf, qbuf, obuf, ostat, ybuf, ystat, cbuf, cstat, zbuf, zstat,
    local_sem, qz_send, qr_send, qy_send, qf_send, q_recv,
    yo_send, ys_send, yo_recv, ys_recv, xo_send, xs_send, zo_send, zs_send, zo_recv, zs_recv,
):
    sec = lax.axis_index("section")
    me = lax.axis_index("kv")
    a = me // inner
    b = me % inner
    following = (sec + 1) % sections
    previous = (sec + sections - 1) % sections
    rows = q_hbm.shape[0]
    depth = k_hbm.shape[0]
    span = q_hbm.shape[1] // HALVES
    heads = H // HALVES

    def cut(hf):
        return pl.ds(hf * span, span)

    table = [line_order(at, outer) for at in range(outer)]

    def outer_at(d):
        at = table[0][d]
        for k in range(1, outer):
            at = jnp.where(a == k, table[k][d], at)
        return at

    def side_of(step):
        return (a + step >= 0) & (a + step < outer)

    def inner_at(e):
        return (b + e) % inner

    loads = [
        pltpu.make_async_copy(k_hbm, kbuf.at[pl.ds(0, depth)], local_sem.at[0]),
        pltpu.make_async_copy(v_hbm, vbuf.at[pl.ds(0, depth)], local_sem.at[1]),
        pltpu.make_async_copy(q_hbm, qbuf.at[me], local_sem.at[2]),
        pltpu.make_async_copy(nk_hbm, nkbuf, local_sem.at[3]),
        pltpu.make_async_copy(nv_hbm, nvbuf, local_sem.at[4]),
    ]
    for load in loads:
        load.start()

    barrier = pltpu.get_barrier_semaphore()
    peers = [(sec, a * inner + inner_at(e)) for e in range(1, inner)]
    peers += [(following, me), (previous, me)]
    for s_at, k_at in peers:
        pl.semaphore_signal(
            barrier, inc=1, device_id={"section": s_at, "kv": k_at}, device_id_type=MESH
        )
    for step in (1, -1):

        @pl.when(side_of(step))
        def _(step=step):
            pl.semaphore_signal(
                barrier, inc=1, device_id={"section": sec, "kv": me + step * inner}, device_id_type=MESH
            )

    lines = side_of(1).astype(jnp.int32) + side_of(-1).astype(jnp.int32)
    pl.semaphore_wait(barrier, len(peers) + lines)

    sends = []

    def push(src, dst, send_sem, recv_sem, s_at, k_at, when=None):
        copy = pltpu.make_async_remote_copy(
            src_ref=src, dst_ref=dst, send_sem=send_sem, recv_sem=recv_sem,
            device_id={"section": s_at, "kv": k_at}, device_id_type=MESH,
        )
        if when is None:
            copy.start()
        else:
            pl.when(when)(copy.start)
        sends.append((copy, when))

    def arrived(dst, recv_sem):
        pltpu.make_async_copy(dst, dst, recv_sem).wait()

    for hf in range(HALVES):
        for e in range(1, inner):
            push(
                q_hbm.at[:, cut(hf)], qbuf.at[me, :, cut(hf)], qy_send.at[e, hf], q_recv.at[me, hf],
                sec, a * inner + inner_at(e),
            )
    for hf in range(HALVES):
        for i, step in enumerate((1, -1)):
            push(
                q_hbm.at[:, cut(hf)], qbuf.at[me, :, cut(hf)], qz_send.at[i, hf], q_recv.at[me, hf],
                sec, jnp.clip(a + step, 0, outer - 1) * inner + b, side_of(step),
            )

    def forward(d, hf):
        zs = outer_at(d)
        slot = zs * inner + b
        piece = qbuf.at[slot, :, cut(hf)]
        arrived(piece, q_recv.at[slot, hf])
        for i, step in enumerate((1, -1)):
            onward = side_of(step) & (zs < a if step > 0 else zs > a)
            push(
                piece, piece, qr_send.at[d, i, hf], q_recv.at[slot, hf],
                sec, jnp.clip(a + step, 0, outer - 1) * inner + b, onward,
            )
        for e in range(1, inner):
            push(
                piece, piece, qf_send.at[d, e, hf], q_recv.at[slot, hf], sec, a * inner + inner_at(e)
            )

    limit = lengths_ref[sec] - me * depth
    place = lax.broadcasted_iota(jnp.int32, (1, depth), 1)
    bias = jnp.where(place < limit, 0.0, NEG).astype(F32)
    scale = (DH ** -0.5) * LOG2E
    count = inner * G * rows
    lane = lax.broadcasted_iota(jnp.int32, (rows, LANES), 1)
    sub = lax.broadcasted_iota(jnp.int32, (rows, LANES), 0)
    ones = jnp.ones((depth + LANES, LANES), BF16)

    def compute(zc, hf):
        own_bias = jnp.concatenate(
            [
                jnp.where(
                    (lane < rows) & (me * rows + lane <= (zc * inner + y) * rows + sub), 0.0, NEG
                ).astype(F32)
                for y in range(inner)
                for _ in range(G)
            ],
            0,
        )

        def one_head(g, stats):
            at = pl.multiple_of(g * DH, DH)
            k = kbuf[:, pl.ds(at, DH)]
            v = vbuf[:, pl.ds(at, DH)]
            q = jnp.concatenate(
                [
                    qbuf[zc * inner + y, :, pl.ds(pl.multiple_of(g * G * DH + h * DH, DH), DH)].astype(F32)
                    for y in range(inner)
                    for h in range(G)
                ],
                0,
            ).astype(BF16)
            s = lax.dot_general(q, k, (((1,), (1,)), ((), ())), preferred_element_type=F32)
            s_old = s[:, :depth] + bias
            s_own = s[:, depth:] + own_bias
            peak = jnp.maximum(
                jnp.max(s_old, axis=-1, keepdims=True), jnp.max(s_own, axis=-1, keepdims=True)
            )
            p = jnp.concatenate(
                [jnp.exp2((s_old - peak) * scale), jnp.exp2((s_own - peak) * scale)], 1
            ).astype(BF16)
            acc = jnp.dot(p, jnp.concatenate([v, ones], 1), preferred_element_type=F32)
            total = acc[:, DH:]
            o = acc[:, :DH] / total
            level = peak * scale + jnp.log2(total)
            stats = list(stats)
            for y in range(inner):
                for h in range(G):
                    base = (y * G + h) * rows
                    obuf[zc * inner + y, :, pl.ds(pl.multiple_of(g * G * DH + h * DH, DH), DH)] = o[
                        base : base + rows
                    ].astype(BF16)
                    stats[y] = jnp.where(lane == g * G + h, level[base : base + rows], stats[y])
            return tuple(stats)

        stats = lax.fori_loop(
            hf * (KVH // HALVES), (hf + 1) * (KVH // HALVES), one_head,
            tuple(jnp.zeros((rows, LANES), F32) for _ in range(inner)), unroll=KVH // HALVES
        )
        for y in range(inner):
            ostat[zc * inner + y, hf] = stats[y]

    def spread(zc, hf):
        for e in range(1, inner):
            target = a * inner + inner_at(e)
            slot = zc * inner + inner_at(e)
            push(
                obuf.at[slot, :, cut(hf)], ybuf.at[zc, b, :, cut(hf)],
                yo_send.at[zc, inner_at(e), hf], yo_recv.at[zc, b, hf], sec, target,
            )
            push(
                ostat.at[slot, hf], ystat.at[zc, b, hf],
                ys_send.at[zc, inner_at(e), hf], ys_recv.at[zc, b, hf], sec, target,
            )

    def deliver(hf):
        for e in range(inner):
            target = a * inner + inner_at(e)
            push(
                obuf.at[target, :, cut(hf)], zbuf.at[outer + b, :, cut(hf)],
                xo_send.at[inner_at(e), hf], zo_recv.at[outer + b, hf], following, target,
            )
            push(
                ostat.at[target, hf], zstat.at[outer + b, hf],
                xs_send.at[inner_at(e), hf], zs_recv.at[outer + b, hf], following, target,
            )

    def mix(hf, parts, levels, store):
        peak = functools.reduce(jnp.maximum, levels)
        shares = [jnp.exp2(level - peak) for level in levels]
        total = functools.reduce(jnp.add, shares)
        shares = [share / total for share in shares]
        for h in range(hf * heads, (hf + 1) * heads):
            cols = pl.ds(h * DH, DH)
            value = functools.reduce(
                jnp.add,
                [part[:, cols].astype(F32) * lane_of(share, h) for part, share in zip(parts, shares)],
            )
            store(cols, value.astype(BF16))
        return peak + jnp.log2(total)

    def combine(zc, hf):
        parts, levels = [obuf.at[zc * inner + b]], [ostat[zc * inner + b, hf]]
        for e in range(1, inner):
            at = inner_at(e)
            arrived(ybuf.at[zc, at, :, cut(hf)], yo_recv.at[zc, at, hf])
            arrived(ystat.at[zc, at, hf], ys_recv.at[zc, at, hf])
            parts.append(ybuf.at[zc, at])
            levels.append(ystat[zc, at, hf])

        def store(cols, value):
            cbuf[zc, :, cols] = value

        cstat[zc, hf] = mix(hf, parts, levels, store)
        target = zc * inner + b
        push(
            cbuf.at[zc, :, cut(hf)], zbuf.at[a, :, cut(hf)], zo_send.at[zc, hf], zo_recv.at[a, hf],
            following, target,
        )
        push(
            cstat.at[zc, hf], zstat.at[a, hf], zs_send.at[zc, hf], zs_recv.at[a, hf],
            following, target,
        )

    def settle():
        for load in loads:
            load.wait()
        pad = jnp.zeros((LANES - rows, kbuf.shape[1]), F32)
        kbuf[pl.ds(depth, LANES), :] = jnp.concatenate([nkbuf[...].astype(F32), pad], 0).astype(BF16)
        vbuf[pl.ds(depth, LANES), :] = jnp.concatenate([nvbuf[...].astype(F32), pad], 0).astype(BF16)

    work = []
    for d in range(1, outer):
        work += [(forward, d, hf) for hf in range(HALVES)]
        if d <= HALVES:
            work.append((None, 0, d - 1))
    work += [(None, 0, hf) for hf in range(outer - 1, HALVES)]
    work += [(None, d, hf) for hf in range(HALVES) for d in range(2, outer)]
    work += [(None, 1, hf) for hf in range(HALVES)]
    done = []
    settled = False
    for act, d, hf in work:
        if act is not None:
            act(d, hf)
            continue
        if not settled:
            settle()
            settled = True
        zc = outer_at(d)
        for e in range(1, inner):
            slot = zc * inner + inner_at(e)
            arrived(qbuf.at[slot, :, cut(hf)], q_recv.at[slot, hf])
        compute(zc, hf)
        if d > 0:
            spread(zc, hf)
            done.append((zc, hf))
            if len(done) > LAG:
                combine(*done.pop(0))
    for hf in range(HALVES):
        deliver(hf)
    for zc, hf in done:
        combine(zc, hf)

    def store_out(cols, value):
        out_ref[:, cols] = value

    origins = [outer_at(d) for d in range(1, outer)] + [outer + y for y in range(inner)]
    for hf in range(HALVES):
        for at in origins:
            arrived(zbuf.at[at, :, cut(hf)], zo_recv.at[at, hf])
            arrived(zstat.at[at, hf], zs_recv.at[at, hf])
        mix(
            hf, [zbuf.at[at] for at in origins], [zstat[at, hf] for at in origins], store_out
        )
    for copy, when in sends:
        if when is None:
            copy.wait_send()
        else:
            pl.when(when)(copy.wait_send)


def split_of(count):
    return 1 << ((count.bit_length() - 1) // 2)


def on_device(sections, count, queries, new_keys, new_values, prefix_keys, prefix_values, lengths):
    inner = split_of(count)
    outer = count // inner
    rows, width = queries.shape
    depth, kv_width = prefix_keys.shape
    vmem = pl.BlockSpec(memory_space=pltpu.VMEM)
    anywhere = pl.BlockSpec(memory_space=pltpu.HBM)
    dma = pltpu.SemaphoreType.DMA
    return pl.pallas_call(
        functools.partial(kernel, sections, outer, inner),
        out_shape=jax.ShapeDtypeStruct((rows, width), BF16),
        in_specs=[pl.BlockSpec(memory_space=pltpu.SMEM), anywhere, anywhere, anywhere, anywhere, anywhere],
        out_specs=vmem,
        scratch_shapes=[
            pltpu.VMEM((rows, kv_width), BF16),
            pltpu.VMEM((rows, kv_width), BF16),
            pltpu.VMEM((depth + LANES, kv_width), BF16),
            pltpu.VMEM((depth + LANES, kv_width), BF16),
            pltpu.VMEM((count, rows, width), BF16),
            pltpu.VMEM((count, rows, width), BF16),
            pltpu.VMEM((count, HALVES, rows, LANES), F32),
            pltpu.VMEM((outer, inner, rows, width), BF16),
            pltpu.VMEM((outer, inner, HALVES, rows, LANES), F32),
            pltpu.VMEM((outer, rows, width), BF16),
            pltpu.VMEM((outer, HALVES, rows, LANES), F32),
            pltpu.VMEM((outer + inner, rows, width), BF16),
            pltpu.VMEM((outer + inner, HALVES, rows, LANES), F32),
            dma((5,)),
            dma((2, HALVES)),
            dma((outer, 2, HALVES)),
            dma((inner, HALVES)),
            dma((outer, inner, HALVES)),
            dma((count, HALVES)),
            dma((outer, inner, HALVES)),
            dma((outer, inner, HALVES)),
            dma((outer, inner, HALVES)),
            dma((outer, inner, HALVES)),
            dma((inner, HALVES)),
            dma((inner, HALVES)),
            dma((outer, HALVES)),
            dma((outer, HALVES)),
            dma((outer + inner, HALVES)),
            dma((outer + inner, HALVES)),
        ],
        compiler_params=pltpu.CompilerParams(
            collective_id=0, has_side_effects=True, vmem_limit_bytes=56 << 20
        ),
        name="section_attention",
    )(lengths, queries, new_keys, new_values, prefix_keys, prefix_values)


def solution(mesh):
    return jax.shard_map(
        functools.partial(on_device, mesh.shape["section"], mesh.shape["kv"]),
        mesh=mesh,
        in_specs=(
            P(("section", "kv"), None),
            P(("section", "kv"), None),
            P(("section", "kv"), None),
            P(("section", "kv"), None),
            P(("section", "kv"), None),
            P(),
        ),
        out_specs=P(("section", "kv"), None),
        check_vma=False,
    )
```
